512 devices in a mesh: prow: 32 (over x, y), pcol: 16 (over z, core).
Axes of the slice: x: 4, y: 8, z: 8, core: 2. Of those that a mesh axis runs over, the one named last changes fastest.
Arguments:
- matrix: bfloat16 [24576, 24576], P('prow', 'pcol'), as said below
- row_pattern: int32 [2, 96], replicated, may hold values from 0 to 1, as said below
- col_pattern: int32 [2, 96], replicated, may hold values from 0 to 1, as said below
Outputs:
- factored: bfloat16 [24576, 24576], P('prow', 'pcol')
The draws below stay inside these ranges and needn't reach their ends.
Inputs may be any that keep to these rules, and one draw needn't show every extreme that they name: 1 where panel k's block column holds nonzeros in block row I, else 0. For each panel, at most 2 of the 3 block rows of any one index of prow are 1, and exactly 2 for some index. row_pattern[1, I] = 1 wherever row_pattern[0, I] = 1. Entries (0, 0) and (1, 3) are 1 and entry (0, 3) is 0. `col_pattern`: 1 where panel k's block row holds nonzeros in block column J, else 0. For each panel, at most 4 of the 6 block columns of any one index of pcol are 1, and exactly 4 for some index. Entries (0, 0), (0, 6) and (1, 6) are 1. `matrix`: in the two pivot blocks (r_k, c_k) every diagonal entry is positive and exceeds the sum of the magnitudes of the other entries of its row by at least one twelfth of itself.
All inputs are finite; a program needn't handle non-finite values.
Results may differ from the reference program's by a relative error of at most 0.0034.
Values may be sent and summed in bfloat16 or wider, within the bound.
No kernel may reach another device: no remote copies, remote signals or barrier semaphores. Data moves between devices by JAX's collectives and lax.ppermute only.
A program may use at most 64 MiB of HBM per device.

```python
import math
import jax
import jax.numpy as jnp
from jax import lax

BLK = 256
RB = 3
CB = 6
ROW_CAP = 2
COL_CAP = 4
ROW_BLOCKS = 96
COL_BLOCKS = 96
ROWS = 24576
COLS = 24576


def pivot_of(key, panel_no):
    key_diag, key_spread, key_cycle = jax.random.split(jax.random.fold_in(key, 100 + panel_no), 3)
    root_size = math.sqrt(BLK)
    diag_vals = jax.random.uniform(key_diag, (BLK,), jnp.float32, 1.5 * root_size, 3.0 * root_size)
    spread_part = jax.random.normal(key_spread, (BLK, BLK), jnp.float32)
    carry_share = 0.85
    spread_share = 0.05
    cycle_order = jax.random.permutation(key_cycle, BLK)
    following = jnp.roll(cycle_order, -1)
    upwind = jnp.zeros((BLK, BLK), jnp.float32).at[cycle_order, following].set(1.0)
    unit_matrix = jnp.eye(BLK, dtype=jnp.float32)
    spread_part = spread_part * (1.0 - unit_matrix) * (1.0 - upwind)
    row_mass = jnp.sum(jnp.abs(spread_part), axis=1) + 1e-06
    spread_part = spread_part * (spread_share * diag_vals / row_mass)[:, None]
    return diag_vals[:, None] * unit_matrix - carry_share * diag_vals[:, None] * upwind + spread_part


def draw_matrix(key, part):
    key_back = jax.random.fold_in(jax.random.fold_in(key, 7), 0)
    background = jax.random.normal(key_back, (ROWS, COLS), jnp.float32)
    for panel_no in range(2):
        background = lax.dynamic_update_slice(background, pivot_of(key, panel_no), (panel_no * RB * BLK, panel_no * CB * BLK))
    return background.astype(jnp.bfloat16)


def ranked(key, slices, slice_width, forced):
    scores = jax.random.randint(key, (slices, slice_width), 0, 1 << 20) * slice_width + jnp.arange(slice_width)[None, :]
    for forced_slice in forced:
        scores = scores.at[forced_slice, 0].set(-1)
    return jnp.argsort(jnp.argsort(scores, axis=1), axis=1).astype(jnp.int32)


def rising_counts(key, slices, capacity):
    steps_along = jnp.arange(slices)
    baseline = 1 + (capacity - 1) * steps_along * steps_along // ((slices - 1) * (slices - 1))
    jitter = jax.random.randint(key, (slices,), -1, 2)
    counts = jnp.clip(baseline + jitter, 1, capacity)
    return counts.at[slices - 1].set(capacity).astype(jnp.int32)


def draw_row_pattern(key, part):
    key_rank, key_count, key_inner = jax.random.split(jax.random.fold_in(key, 11), 3)
    slices = ROW_BLOCKS // RB
    priority = ranked(key_rank, slices, RB, (0, 1))
    outer_count = rising_counts(key_count, slices, ROW_CAP)
    inner_count = jax.random.randint(key_inner, (slices,), 0, 1 << 16) % outer_count + 1
    inner_count = inner_count.at[slices - 1].set(ROW_CAP)
    second_panel = (priority < outer_count[:, None]).reshape(ROW_BLOCKS)
    first_panel = (priority < inner_count[:, None]).reshape(ROW_BLOCKS).at[RB].set(False)
    return jnp.stack([first_panel, second_panel]).astype(jnp.int32)


def draw_col_pattern(key, part):
    key_first, key_second, key_count_a, key_count_b = jax.random.split(jax.random.fold_in(key, 13), 4)
    slices = COL_BLOCKS // CB
    first_rank = ranked(key_first, slices, CB, (0, 1))
    second_rank = ranked(key_second, slices, CB, (1,))
    first_count = rising_counts(key_count_a, slices, COL_CAP)
    second_count = rising_counts(key_count_b, slices, COL_CAP)
    first_panel = (first_rank < first_count[:, None]).reshape(COL_BLOCKS)
    second_panel = (second_rank < second_count[:, None]).reshape(COL_BLOCKS)
    return jnp.stack([first_panel, second_panel]).astype(jnp.int32)


def setup_inputs(seed: int = 0) -> dict:
    key_list = jax.random.split(jax.random.key(seed), 4)
    matrix = draw_matrix(jax.random.fold_in(key_list[3], 71), 0)
    row_pattern = draw_row_pattern(jax.random.fold_in(key_list[3], 71), 0)
    col_pattern = draw_col_pattern(jax.random.fold_in(key_list[3], 71), 0)
    return {"matrix": matrix, "row_pattern": row_pattern, "col_pattern": col_pattern}


def reference(matrix, row_pattern, col_pattern):
    row_keep = jnp.repeat(row_pattern, BLK, axis=1) > 0
    col_keep = jnp.repeat(col_pattern, BLK, axis=1) > 0
    zero_value = jnp.zeros((), matrix.dtype)
    for panel_no in range(2):
        row_start = panel_no * RB * BLK
        col_start = panel_no * CB * BLK
        column_part = matrix[:, col_start:col_start + BLK]
        matrix = matrix.at[:, col_start:col_start + BLK].set(jnp.where(row_keep[panel_no][:, None], column_part, zero_value))
        row_part = matrix[row_start:row_start + BLK, :]
        matrix = matrix.at[row_start:row_start + BLK, :].set(jnp.where(col_keep[panel_no][None, :], row_part, zero_value))
    positions = jnp.arange(ROWS)
    col_positions = jnp.arange(COLS)
    row_done = jnp.zeros((ROWS,), dtype=jnp.bool_)
    col_done = jnp.zeros((COLS,), dtype=jnp.bool_)
    for panel_no in range(2):
        row_start = panel_no * RB * BLK
        col_start = panel_no * CB * BLK
        row_done = row_done | (positions >= row_start) & (positions < row_start + BLK)
        col_done = col_done | (col_positions >= col_start) & (col_positions < col_start + BLK)
        pivot_block = matrix[row_start:row_start + BLK, col_start:col_start + BLK].astype(jnp.float32)
        inverse = jnp.linalg.solve(pivot_block, jnp.eye(BLK, dtype=jnp.float32))
        factor = jnp.dot(matrix[:, col_start:col_start + BLK].astype(jnp.float32), inverse, precision=lax.Precision.HIGHEST)
        factor = jnp.where(row_done[:, None], jnp.zeros((), factor.dtype), factor).astype(jnp.bfloat16)
        upper_part = jnp.where(col_done[None, :], jnp.zeros((), matrix.dtype), matrix[row_start:row_start + BLK, :])

        def strip_update(operands):
            source, lower_rows = operands
            return (source.astype(jnp.float32) - jnp.dot(lower_rows.astype(jnp.float32), upper_part.astype(jnp.float32), preferred_element_type=jnp.float32)).astype(jnp.bfloat16)
        strips = lax.map(strip_update, (matrix.reshape(ROWS // BLK, BLK, COLS), factor.reshape(ROWS // BLK, BLK, BLK)))
        matrix = strips.reshape(ROWS, COLS)
        column_part = matrix[:, col_start:col_start + BLK]
        matrix = matrix.at[:, col_start:col_start + BLK].set(jnp.where(row_done[:, None], column_part, factor))
    return matrix
```

```python
import jax
import jax.numpy as jnp
from jax import lax
from jax.experimental import pallas as pl
from jax.experimental.pallas import tpu as pltpu
from jax.sharding import Mesh
from jax.sharding import PartitionSpec as P

BLK = 256
X, Y, Z = 4, 8, 8
AXES = ("prow_0", "prow_1", "pcol")
PROW = ("prow_0", "prow_1")
ROW_CAP, COL_CAP = 2, 4


def device(x, y, z, core):
    return ((x % X) * Y + y % Y) * (2 * Z) + (z % Z) * 2 + core


def plane_pairs(pairs):
    out = []
    for (xs, ys), (xt, yt) in pairs:
        for z in range(Z):
            for core in range(2):
                out.append((device(xs, ys, z, core), device(xt, yt, z, core)))
                out.append((device(xs, 1 - ys, z, core), device(xt, 1 - yt, z, core)))
    return out


def line_pairs(pairs):
    return [
        (device(x, y, s, core), device(x, y, t, core))
        for s, t in pairs
        for x in range(X)
        for y in range(Y)
        for core in range(2)
    ]


HOLDERS = [(0, 0), (2, 0), (1, 4), (3, 4)]
SPREAD_1 = [plane_pairs([((0, 0), h)]) for h in ((3, 4), (1, 4), (2, 0))]
SPREAD_2 = [
    plane_pairs([(h, (h[0] + dx, h[1] + dy)) for h in HOLDERS])
    for dx, dy in ((-1, 2), (0, 2), (1, 0))
]
UP = [
    (device(x, y, z, c), device(x, y + 1, z, c))
    for x in range(X) for y in range(Y) for z in range(Z) for c in range(2)
]
DOWN = [(t, s) for s, t in UP]
LINE_1 = [line_pairs([(0, 3)]), line_pairs([(0, 5)])]
LINE_2 = [line_pairs([(0, 1), (3, 4), (5, 6)]), line_pairs([(0, 7), (3, 2)])]
SWAP = [
    (device(x, y, z, c), device(x, y, z, 1 - c))
    for x in range(X) for y in range(Y) for z in range(Z) for c in range(2)
]


def send(value, pairs):
    return lax.ppermute(value, AXES, pairs)


def slots(flags, capacity):
    count = jnp.int32(0)
    slot_of = []
    where = [jnp.int32(0)] * capacity
    for position, flag in enumerate(flags):
        one = flag.astype(jnp.int32)
        slot_of.append(jnp.minimum(count, capacity - 1))
        where = [
            jnp.where(flag & (count == s), jnp.int32(position), w) for s, w in enumerate(where)
        ]
        count = count + one
    return slot_of, where, count


def pack_kernel(here, row_pattern, col_pattern, matrix, first_out, rest_out, panel_out, sems):
    prow, pcol = here[0], here[1]
    row_blocks, col_blocks = matrix.shape[0] // BLK, matrix.shape[1] // BLK
    k = (prow == 1).astype(jnp.int32)
    cols = [col_pattern[k, pcol * col_blocks + j] > 0 for j in range(col_blocks)]
    _, col_at, _ = slots(cols, COL_CAP)
    copies = []
    for s in range(COL_CAP):
        source = matrix.at[pl.ds(0, BLK), pl.ds(pl.multiple_of(col_at[s] * BLK, BLK), BLK)]
        target = first_out if s == 0 else rest_out.at[pl.ds((s - 1) * BLK, BLK)]
        copies.append(pltpu.make_async_copy(source, target, sems.at[s]))
    rows = [row_pattern[1, prow * row_blocks + i] > 0 for i in range(row_blocks)]
    _, row_at, count = slots(rows, ROW_CAP)
    for s in range(ROW_CAP):
        source = matrix.at[pl.ds(pl.multiple_of(row_at[s] * BLK, BLK), BLK), pl.ds(0, BLK)]
        target = panel_out.at[pl.ds(s * BLK, BLK)]
        copies.append(pltpu.make_async_copy(source, target, sems.at[COL_CAP + s]))
    for copy in copies:
        copy.start()
    for copy in copies:
        copy.wait()
    own = (pcol == 1).astype(jnp.int32)
    for s in range(ROW_CAP):
        stored = (count > s) & (row_pattern[own, prow * row_blocks + row_at[s]] > 0)

        @pl.when(jnp.logical_not(stored))
        def _(s=s):
            panel_out[pl.ds(s * BLK, BLK), :] = jnp.zeros((BLK, BLK), jnp.bfloat16)


def pack(here, row_pattern, col_pattern, matrix):
    smem = pl.BlockSpec(memory_space=pltpu.SMEM)
    vmem = pl.BlockSpec(memory_space=pltpu.VMEM)
    return pl.pallas_call(
        pack_kernel,
        in_specs=[smem, smem, smem, pl.BlockSpec(memory_space=pl.ANY)],
        out_specs=[vmem] * 3,
        out_shape=[
            jax.ShapeDtypeStruct((BLK, BLK), jnp.bfloat16),
            jax.ShapeDtypeStruct(((COL_CAP - 1) * BLK, BLK), jnp.bfloat16),
            jax.ShapeDtypeStruct((ROW_CAP * BLK, BLK), jnp.bfloat16),
        ],
        scratch_shapes=[pltpu.SemaphoreType.DMA((COL_CAP + ROW_CAP,))],
        name="pack",
    )(here, row_pattern, col_pattern, matrix)


def halves(value):
    high = value.astype(jnp.bfloat16)
    return high, (value - high.astype(jnp.float32)).astype(jnp.bfloat16)


def dot(a, b):
    return jnp.dot(a, b, preferred_element_type=jnp.float32)


def panels_kernel(
    here, row_pattern, pivot_0, upper_01, pivot_1, panel_0, panel_1, lower_0, lower_1
):
    prow = here[0]
    row_blocks = row_pattern.shape[1] // (X * Y)
    i = lax.broadcasted_iota(jnp.int32, (BLK, BLK), 0)
    j = lax.broadcasted_iota(jnp.int32, (BLK, BLK), 1)
    diagonal = i == j
    powers, sums, scales = [], [], []
    for pivot in (pivot_0, pivot_1):
        p = pivot[...].astype(jnp.float32)
        d = jnp.where(diagonal, p, 0.0)
        by_row = jnp.sum(d, axis=1, keepdims=True)
        scales.append(1.0 / jnp.sum(d, axis=0, keepdims=True))
        r = jnp.where(diagonal, 0.0, -p / by_row)
        powers.append(r)
        sums.append(jnp.where(diagonal, 1.0, r))
    for step in range(8):
        for n in range(2):
            high, low = halves(powers[n])
            if step > 0:
                sum_high, sum_low = halves(sums[n])
                sums[n] = sums[n] + (
                    dot(high, sum_high) + (dot(high, sum_low) + dot(low, sum_high))
                )
            if step < 7:
                powers[n] = dot(high, high) + (dot(high, low) + dot(low, high))
    rows = [row_pattern[1, prow * row_blocks + b] > 0 for b in range(row_blocks)]
    _, row_at, _ = slots(rows, ROW_CAP)
    for n in range(2):
        inverse = sums[n] * scales[n]
        high, low = halves(inverse)
        for s in range(ROW_CAP):
            here_rows = pl.ds(s * BLK, BLK)
            if n == 0:
                source = panel_0[here_rows, :]
                done = (prow == 0) & (row_at[s] == 0)
            else:
                source = (
                    panel_1[here_rows, :].astype(jnp.float32)
                    - dot(lower_0[here_rows, :], upper_01[...])
                ).astype(jnp.bfloat16)
                done = (prow <= 1) & (row_at[s] == 0)
            lower = dot(source, high) + dot(source, low)
            target = lower_0 if n == 0 else lower_1
            target[here_rows, :] = jnp.where(done, 0.0, lower).astype(jnp.bfloat16)


def panels(here, row_pattern, *blocks):
    smem = pl.BlockSpec(memory_space=pltpu.SMEM)
    vmem = pl.BlockSpec(memory_space=pltpu.VMEM)
    shape = jax.ShapeDtypeStruct((ROW_CAP * BLK, BLK), jnp.bfloat16)
    return pl.pallas_call(
        panels_kernel,
        in_specs=[smem, smem] + [vmem] * 5,
        out_specs=[vmem] * 2,
        out_shape=[shape, shape],
        name="panels",
    )(here, row_pattern, *blocks)


def update_kernel(
    here, row_pattern, col_pattern, source, lower_0, lower_1, first_0, rest_0, first_1, rest_1, out
):
    prow, pcol = here[0], here[1]
    i = pl.program_id(0)
    row_blocks = pl.num_programs(0)
    col_blocks = source.shape[1] // BLK
    row = prow * row_blocks + i
    slot = jnp.int32(0)
    for b in range(2):
        slot = slot + ((i > b) & (row_pattern[1, prow * row_blocks + b] > 0)).astype(jnp.int32)
    slot = jnp.minimum(slot, ROW_CAP - 1)
    stored = [row_pattern[k, row] > 0 for k in range(2)]
    first = i == 0
    done = [first & (prow == 0), first & (prow <= 1)]
    rows = pl.ds(pl.multiple_of(slot * BLK, BLK), BLK)
    lower = [lower_0[rows, :], lower_1[rows, :]]
    upper = [(first_0, rest_0), (first_1, rest_1)]
    flags = [[col_pattern[k, pcol * col_blocks + j] > 0 for j in range(col_blocks)] for k in (0, 1)]
    col_slot = [slots(f, COL_CAP)[0] for f in flags]
    for j in range(col_blocks):
        columns = pl.ds(j * BLK, BLK)
        dropped = jnp.bool_(False)
        for k in range(2):
            dropped = dropped | (first & (prow == k) & jnp.logical_not(flags[k][j]))
            if j == 0:
                dropped = dropped | ((pcol == k) & jnp.logical_not(stored[k]))
        value = jnp.where(dropped, 0.0, source[:, columns].astype(jnp.float32))
        for k in range(2):
            used = stored[k] & jnp.logical_not(done[k]) & flags[k][j]
            if j == 0:
                used = used & (pcol > k)
            s = col_slot[k][j]
            if j == 0:
                block = upper[k][0][...]
            else:
                at = pl.ds(pl.multiple_of(jnp.maximum(s - 1, 0) * BLK, BLK), BLK)
                block = jnp.where(s == 0, upper[k][0][...], upper[k][1][at, :])
            product = jnp.where(used, dot(lower[k], block), 0.0)
            value = (value - product).astype(jnp.bfloat16)
            if j == 0:
                taken = (pcol == k) & jnp.logical_not(done[k])
                kept = jnp.where(stored[k], lower[k], jnp.zeros_like(lower[k]))
                value = jnp.where(taken, kept, value)
            if k == 0:
                value = value.astype(jnp.float32)
        out[:, columns] = value


def update(here, row_pattern, col_pattern, matrix, *blocks):
    row_blocks = matrix.shape[0] // BLK
    breadth = matrix.shape[1]
    smem = pl.BlockSpec(memory_space=pltpu.SMEM)
    vmem = pl.BlockSpec(memory_space=pltpu.VMEM)
    strip = pl.BlockSpec((BLK, breadth), lambda i: (i, 0))
    return pl.pallas_call(
        update_kernel,
        grid=(row_blocks,),
        in_specs=[smem] * 3 + [strip] + [vmem] * 6,
        out_specs=strip,
        out_shape=jax.ShapeDtypeStruct(matrix.shape, matrix.dtype),
        name="update",
    )(here, row_pattern, col_pattern, matrix, *blocks)


def shards(matrix, row_pattern, col_pattern):
    prow = lax.axis_index(PROW).astype(jnp.int32)
    pcol = lax.axis_index("pcol").astype(jnp.int32)
    y = lax.axis_index("prow_1")
    here = jnp.where(jnp.arange(2) == 0, prow, pcol)
    even = y % 2 == 0
    core_0 = pcol % 2 == 0
    first, rest, panel = pack(here, row_pattern, col_pattern, matrix)
    zero = jnp.zeros((), jnp.bfloat16)

    def only(flag, value):
        return jnp.where(flag, value, zero)

    def spread(value):
        held = only(prow <= 1, value)
        for pairs in SPREAD_1:
            held = held + send(value, pairs)
        every = held
        for pairs in SPREAD_2:
            every = every + send(held, pairs)
        return every

    def along(value):
        held = only(pcol <= 1, value)
        for pairs in LINE_1:
            held = held + send(value, pairs)
        every = held
        for pairs in LINE_2:
            every = every + send(held, pairs)
        return every, send(every, SWAP)

    first_held = spread(first)
    first_came = send(first_held, UP)
    first_0 = jnp.where(even, first_held, first_came)
    first_1 = jnp.where(even, first_came, first_held)
    mine, other = along(panel)
    panel_0 = jnp.where(core_0, mine, other)
    panel_1 = jnp.where(core_0, other, mine)
    mine, other = along(jnp.concatenate([first_0, first_1], axis=0))
    pivot_0 = jnp.where(core_0, mine[:BLK], other[:BLK])
    upper_01 = jnp.where(core_0, other[:BLK], mine[:BLK])
    pivot_1 = jnp.where(core_0, other[BLK:], mine[BLK:])
    rest_held = spread(rest)
    half = rest.shape[0] // 2
    rest_came = jnp.concatenate(
        [send(rest_held[:half], UP), send(rest_held[half:], DOWN)],
        axis=0,
    )
    rest_0 = jnp.where(even, rest_held, rest_came)
    rest_1 = jnp.where(even, rest_came, rest_held)
    lower_0, lower_1 = panels(here, row_pattern, pivot_0, upper_01, pivot_1, panel_0, panel_1)
    return update(
        here, row_pattern, col_pattern, matrix,
        lower_0, lower_1, first_0, rest_0, first_1, rest_1,
    )


def solution(mesh):
    torus = Mesh(mesh.devices.reshape(X, Y, mesh.shape["pcol"]), AXES)
    placed = (P(PROW, "pcol"), P(), P())
    return jax.shard_map(
        shards, mesh=torus, in_specs=placed, out_specs=P(PROW, "pcol"), check_vma=False
    )
```

```python
import jax
import jax.numpy as jnp
from jax import lax
from jax.experimental import pallas as pl
from jax.experimental.pallas import tpu as pltpu
from jax.sharding import Mesh
from jax.sharding import PartitionSpec as P


BLK = 256
X, Y, Z = 4, 8, 8
AXES = ("prow_0", "prow_1", "pcol")
PROW = ("prow_0", "prow_1")
ROW_CAP, COL_CAP = 2, 4


def device(x, y, z, core):
    return ((x % X) * Y + y % Y) * (2 * Z) + (z % Z) * 2 + core


def plane_pairs(pairs):
    out = []
    for (xs, ys), (xt, yt) in pairs:
        for z in range(Z):
            for core in range(2):
                out.append((device(xs, ys, z, core), device(xt, yt, z, core)))
                out.append((device(xs, 1 - ys, z, core), device(xt, 1 - yt, z, core)))
    return out


def line_pairs(pairs):
    return [
        (device(x, y, s, core), device(x, y, t, core))
        for s, t in pairs
        for x in range(X)
        for y in range(Y)
        for core in range(2)
    ]


HOLDERS = [(0, 0), (1, 6), (3, 2), (0, 6)]
SPREAD_1 = [plane_pairs([((0, 0), h)]) for h in HOLDERS[1:]]
TARGETS = [
    [(2, 0), (1, 4), (2, 2), (2, 4)],
    [(1, 2), (1, 0), (3, 4), (0, 4)],
    [(3, 0), (2, 6), (0, 2), (3, 6)],
]
SPREAD_2 = [plane_pairs(list(zip(HOLDERS, targets))) for targets in TARGETS]
UP = [
    (device(x, y, z, c), device(x, y + 1, z, c))
    for x in range(X) for y in range(Y) for z in range(Z) for c in range(2)
]
DOWN = [(t, s) for s, t in UP]
LINE_1 = [line_pairs([(0, 3)]), line_pairs([(0, 5)])]
LINE_2 = [line_pairs([(0, 1), (3, 4), (5, 6)]), line_pairs([(0, 7), (3, 2)])]
SWAP = [
    (device(x, y, z, c), device(x, y, z, 1 - c))
    for x in range(X) for y in range(Y) for z in range(Z) for c in range(2)
]


def send(value, pairs):
    return lax.ppermute(value, AXES, pairs)


def slots(flags, capacity):
    count = jnp.int32(0)
    slot_of = []
    where = [jnp.int32(0)] * capacity
    for position, flag in enumerate(flags):
        one = flag.astype(jnp.int32)
        slot_of.append(jnp.minimum(count, capacity - 1))
        where = [
            jnp.where(flag & (count == s), jnp.int32(position), w) for s, w in enumerate(where)
        ]
        count = count + one
    return slot_of, where, count


def pack_kernel(here, row_pattern, col_pattern, matrix, upper_out, panel_out, sems):
    prow, pcol = here[0], here[1]
    row_blocks, col_blocks = matrix.shape[0] // BLK, matrix.shape[1] // BLK
    k = (prow == 1).astype(jnp.int32)
    cols = [col_pattern[k, pcol * col_blocks + j] > 0 for j in range(col_blocks)]
    _, col_at, _ = slots(cols, COL_CAP)
    copies = []
    for s in range(COL_CAP):
        source = matrix.at[pl.ds(0, BLK), pl.ds(pl.multiple_of(col_at[s] * BLK, BLK), BLK)]
        target = upper_out.at[pl.ds(s * BLK, BLK)]
        copies.append(pltpu.make_async_copy(source, target, sems.at[s]))
    rows = [row_pattern[1, prow * row_blocks + i] > 0 for i in range(row_blocks)]
    _, row_at, count = slots(rows, ROW_CAP)
    for s in range(ROW_CAP):
        source = matrix.at[pl.ds(pl.multiple_of(row_at[s] * BLK, BLK), BLK), pl.ds(0, BLK)]
        target = panel_out.at[pl.ds(s * BLK, BLK)]
        copies.append(pltpu.make_async_copy(source, target, sems.at[COL_CAP + s]))
    for copy in copies:
        copy.start()
    for copy in copies:
        copy.wait()
    own = (pcol == 1).astype(jnp.int32)
    for s in range(ROW_CAP):
        stored = (count > s) & (row_pattern[own, prow * row_blocks + row_at[s]] > 0)

        @pl.when(jnp.logical_not(stored))
        def _(s=s):
            panel_out[pl.ds(s * BLK, BLK), :] = jnp.zeros((BLK, BLK), jnp.bfloat16)


def pack(here, row_pattern, col_pattern, matrix):
    smem = pl.BlockSpec(memory_space=pltpu.SMEM)
    vmem = pl.BlockSpec(memory_space=pltpu.VMEM)
    return pl.pallas_call(
        pack_kernel,
        in_specs=[smem, smem, smem, pl.BlockSpec(memory_space=pl.ANY)],
        out_specs=[vmem] * 2,
        out_shape=[
            jax.ShapeDtypeStruct((COL_CAP * BLK, BLK), jnp.bfloat16),
            jax.ShapeDtypeStruct((ROW_CAP * BLK, BLK), jnp.bfloat16),
        ],
        scratch_shapes=[pltpu.SemaphoreType.DMA((COL_CAP + ROW_CAP,))],
        name="pack",
    )(here, row_pattern, col_pattern, matrix)


def halves(value):
    high = value.astype(jnp.bfloat16)
    return high, (value - high.astype(jnp.float32)).astype(jnp.bfloat16)


def dot(a, b):
    return jnp.dot(a, b, preferred_element_type=jnp.float32)


def invert_kernel(pivot_0, pivot_1, *out):
    i = lax.broadcasted_iota(jnp.int32, (BLK, BLK), 0)
    j = lax.broadcasted_iota(jnp.int32, (BLK, BLK), 1)
    diagonal = i == j
    powers, sums, scales = [], [], []
    for pivot in (pivot_0, pivot_1):
        p = pivot[...].astype(jnp.float32)
        d = jnp.where(diagonal, p, 0.0)
        by_row = jnp.sum(d, axis=1, keepdims=True)
        scales.append(1.0 / jnp.sum(d, axis=0, keepdims=True))
        r = jnp.where(diagonal, 0.0, -p / by_row)
        powers.append(r)
        sums.append(jnp.where(diagonal, 1.0, r))
    for step in range(8):
        for n in range(2):
            high, low = halves(powers[n])
            if step > 0:
                sum_high, sum_low = halves(sums[n])
                sums[n] = sums[n] + (
                    dot(high, sum_high) + (dot(high, sum_low) + dot(low, sum_high))
                )
            if step < 7:
                powers[n] = dot(high, high) + (dot(high, low) + dot(low, high))
    for n in range(2):
        high, low = halves(sums[n] * scales[n])
        out[2 * n][...] = high
        out[2 * n + 1][...] = low


def invert(pivot_0, pivot_1):
    vmem = pl.BlockSpec(memory_space=pltpu.VMEM)
    return pl.pallas_call(
        invert_kernel,
        in_specs=[vmem] * 2,
        out_specs=[vmem] * 4,
        out_shape=[jax.ShapeDtypeStruct((BLK, BLK), jnp.bfloat16)] * 4,
        cost_estimate=pl.CostEstimate(
            flops=96 * BLK**3, bytes_accessed=12 * BLK * BLK, transcendentals=0
        ),
        name="invert",
    )(pivot_0, pivot_1)


def lower_kernel(
    here, row_pattern, high_0, low_0, high_1, low_1, upper_01, panel_0, panel_1, lower_0, lower_1
):
    prow = here[0]
    row_blocks = row_pattern.shape[1] // (X * Y)
    rows = [row_pattern[1, prow * row_blocks + b] > 0 for b in range(row_blocks)]
    _, row_at, _ = slots(rows, ROW_CAP)
    for s in range(ROW_CAP):
        at = pl.ds(s * BLK, BLK)
        lower = dot(panel_0[at, :], high_0[...]) + dot(panel_0[at, :], low_0[...])
        done = (prow == 0) & (row_at[s] == 0)
        lower = jnp.where(done, 0.0, lower).astype(jnp.bfloat16)
        lower_0[at, :] = lower
        rest = panel_1[at, :].astype(jnp.float32) - dot(lower, upper_01[...])
        rest = rest.astype(jnp.bfloat16)
        lower = dot(rest, high_1[...]) + dot(rest, low_1[...])
        done = (prow <= 1) & (row_at[s] == 0)
        lower_1[at, :] = jnp.where(done, 0.0, lower).astype(jnp.bfloat16)


def lowers(here, row_pattern, *blocks):
    smem = pl.BlockSpec(memory_space=pltpu.SMEM)
    vmem = pl.BlockSpec(memory_space=pltpu.VMEM)
    shape = jax.ShapeDtypeStruct((ROW_CAP * BLK, BLK), jnp.bfloat16)
    return pl.pallas_call(
        lower_kernel,
        in_specs=[smem, smem] + [vmem] * 7,
        out_specs=[vmem] * 2,
        out_shape=[shape, shape],
        name="lowers",
    )(here, row_pattern, *blocks)


def update_kernel(
    here, row_pattern, col_pattern, source, lower_0, lower_1, upper_0, upper_1, out
):
    prow, pcol = here[0], here[1]
    i = pl.program_id(0)
    row_blocks = pl.num_programs(0)
    col_blocks = source.shape[1] // BLK
    row = prow * row_blocks + i
    slot = jnp.int32(0)
    for b in range(2):
        slot = slot + ((i > b) & (row_pattern[1, prow * row_blocks + b] > 0)).astype(jnp.int32)
    slot = jnp.minimum(slot, ROW_CAP - 1)
    stored = [row_pattern[k, row] > 0 for k in range(2)]
    first = i == 0
    done = [first & (prow == 0), first & (prow <= 1)]
    rows = pl.ds(pl.multiple_of(slot * BLK, BLK), BLK)
    lower = [lower_0[rows, :], lower_1[rows, :]]
    upper = [upper_0, upper_1]
    flags = [[col_pattern[k, pcol * col_blocks + j] > 0 for j in range(col_blocks)] for k in (0, 1)]
    col_slot = [slots(f, COL_CAP)[0] for f in flags]
    for j in range(col_blocks):
        columns = pl.ds(j * BLK, BLK)
        dropped = jnp.bool_(False)
        for k in range(2):
            dropped = dropped | (first & (prow == k) & jnp.logical_not(flags[k][j]))
            if j == 0:
                dropped = dropped | ((pcol == k) & jnp.logical_not(stored[k]))
        value = jnp.where(dropped, 0.0, source[:, columns].astype(jnp.float32))
        for k in range(2):
            used = stored[k] & jnp.logical_not(done[k]) & flags[k][j]
            if j == 0:
                used = used & (pcol > k)
            at = pl.ds(pl.multiple_of(col_slot[k][j] * BLK, BLK), BLK)
            block = upper[k][at, :]
            product = jnp.where(used, dot(lower[k], block), 0.0)
            value = (value - product).astype(jnp.bfloat16)
            if j == 0:
                taken = (pcol == k) & jnp.logical_not(done[k])
                kept = jnp.where(stored[k], lower[k], jnp.zeros_like(lower[k]))
                value = jnp.where(taken, kept, value)
            if k == 0:
                value = value.astype(jnp.float32)
        out[:, columns] = value


def update(here, row_pattern, col_pattern, matrix, *blocks):
    row_blocks = matrix.shape[0] // BLK
    breadth = matrix.shape[1]
    smem = pl.BlockSpec(memory_space=pltpu.SMEM)
    vmem = pl.BlockSpec(memory_space=pltpu.VMEM)
    strip = pl.BlockSpec((BLK, breadth), lambda i: (i, 0))
    return pl.pallas_call(
        update_kernel,
        grid=(row_blocks,),
        in_specs=[smem] * 3 + [strip] + [vmem] * 4,
        out_specs=strip,
        out_shape=jax.ShapeDtypeStruct(matrix.shape, matrix.dtype),
        name="update",
    )(here, row_pattern, col_pattern, matrix, *blocks)


def shards(matrix, row_pattern, col_pattern):
    prow = lax.axis_index(PROW).astype(jnp.int32)
    pcol = lax.axis_index("pcol").astype(jnp.int32)
    y = lax.axis_index("prow_1")
    here = jnp.where(jnp.arange(2) == 0, prow, pcol)
    even = y % 2 == 0
    core_0 = pcol % 2 == 0
    upper, panel = pack(here, row_pattern, col_pattern, matrix)
    zero = jnp.zeros((), jnp.bfloat16)

    def only(flag, value):
        return jnp.where(flag, value, zero)

    def spread(value):
        held = only(prow <= 1, value)
        for pairs in SPREAD_1:
            held = held + send(value, pairs)
        every = held
        for pairs in SPREAD_2:
            every = every + send(held, pairs)
        return every

    def along(value):
        held = only(pcol <= 1, value)
        for pairs in LINE_1:
            held = held + send(value, pairs)
        every = held
        for pairs in LINE_2:
            every = every + send(held, pairs)
        return every

    upper_held = spread(upper)
    half = upper.shape[0] // 2
    upper_came = jnp.concatenate(
        [send(upper_held[:half], UP), send(upper_held[half:], DOWN)],
        axis=0,
    )
    upper_0 = jnp.where(even, upper_held, upper_came)
    upper_1 = jnp.where(even, upper_came, upper_held)
    panel = along(panel)
    pivot_held = spread(panel[:BLK])
    pivot_came = send(pivot_held, UP)
    mine = jnp.concatenate(
        [jnp.where(even, pivot_held, pivot_came), jnp.where(even, pivot_came, pivot_held), panel],
        axis=0,
    )
    other = send(mine, SWAP)
    pivot_0 = jnp.where(core_0, mine[:BLK], other[:BLK])
    pivot_1 = jnp.where(core_0, other[BLK : 2 * BLK], mine[BLK : 2 * BLK])
    upper_01 = jnp.where(core_0, other[:BLK], mine[:BLK])
    panel_0 = jnp.where(core_0, mine[2 * BLK :], other[2 * BLK :])
    panel_1 = jnp.where(core_0, other[2 * BLK :], mine[2 * BLK :])
    inverses = invert(pivot_0, pivot_1)
    lower_0, lower_1 = lowers(here, row_pattern, *inverses, upper_01, panel_0, panel_1)
    return update(
        here, row_pattern, col_pattern, matrix, lower_0, lower_1, upper_0, upper_1
    )


def solution(mesh):
    torus = Mesh(mesh.devices.reshape(X, Y, mesh.shape["pcol"]), AXES)
    placed = (P(PROW, "pcol"), P(), P())
    return jax.shard_map(
        shards, mesh=torus, in_specs=placed, out_specs=P(PROW, "pcol"), check_vma=False
    )
```

```python
import jax
import jax.numpy as jnp
from jax import lax
from jax.experimental import pallas as pl
from jax.experimental.pallas import tpu as pltpu
from jax.sharding import Mesh
from jax.sharding import PartitionSpec as P


BLK = 256
X, Y, Z = 4, 8, 8
AXES = ("prow_0", "prow_1", "pcol")
PROW = ("prow_0", "prow_1")
ROW_CAP, COL_CAP = 2, 4


def device(x, y, z, core):
    return ((x % X) * Y + y % Y) * (2 * Z) + (z % Z) * 2 + core


def plane_pairs(pairs):
    out = []
    for (xs, ys), (xt, yt) in pairs:
        for z in range(Z):
            for core in range(2):
                out.append((device(xs, ys, z, core), device(xt, yt, z, core)))
                out.append((device(xs, 1 - ys, z, core), device(xt, 1 - yt, z, core)))
    return out


def line_pairs(pairs):
    return [
        (device(x, y, s, core), device(x, y, t, core))
        for s, t in pairs
        for x in range(X)
        for y in range(Y)
        for core in range(2)
    ]


SPREAD = [
    [plane_pairs([((0, 0), h)]) for h in ((2, 6), (1, 0), (3, 0))],
    [plane_pairs([((0, 0), (0, 6)), ((1, 0), (1, 6)), ((3, 0), (3, 6)), ((2, 6), (2, 0))])],
    [plane_pairs([((x, 0), (x, 2)) for x in range(X)] + [((x, 6), (x, 4)) for x in range(X)])],
]
UP = [
    (device(x, y, z, c), device(x, y + 1, z, c))
    for x in range(X) for y in range(Y) for z in range(Z) for c in range(2)
]
DOWN = [(t, s) for s, t in UP]
LINE_1 = [line_pairs([(0, 3)]), line_pairs([(0, 5)])]
LINE_2 = [line_pairs([(0, 1), (3, 4), (5, 6)]), line_pairs([(0, 7), (3, 2)])]
SWAP = [
    (device(x, y, z, c), device(x, y, z, 1 - c))
    for x in range(X) for y in range(Y) for z in range(Z) for c in range(2)
]


def send(value, pairs):
    return lax.ppermute(value, AXES, pairs)


def slots(flags, capacity):
    count = jnp.int32(0)
    slot_of = []
    where = [jnp.int32(0)] * capacity
    for position, flag in enumerate(flags):
        one = flag.astype(jnp.int32)
        slot_of.append(jnp.minimum(count, capacity - 1))
        where = [
            jnp.where(flag & (count == s), jnp.int32(position), w) for s, w in enumerate(where)
        ]
        count = count + one
    return slot_of, where, count


def pack_kernel(here, row_pattern, col_pattern, matrix, first_out, rest_out, panel_out, sems):
    prow, pcol = here[0], here[1]
    row_blocks, col_blocks = matrix.shape[0] // BLK, matrix.shape[1] // BLK
    k = (prow == 1).astype(jnp.int32)
    cols = [col_pattern[k, pcol * col_blocks + j] > 0 for j in range(col_blocks)]
    _, col_at, _ = slots(cols, COL_CAP)
    copies = []
    for s in range(COL_CAP):
        source = matrix.at[pl.ds(0, BLK), pl.ds(pl.multiple_of(col_at[s] * BLK, BLK), BLK)]
        target = first_out if s == 0 else rest_out.at[pl.ds((s - 1) * BLK, BLK)]
        copies.append(pltpu.make_async_copy(source, target, sems.at[s]))
    rows = [row_pattern[1, prow * row_blocks + i] > 0 for i in range(row_blocks)]
    _, row_at, count = slots(rows, ROW_CAP)
    for s in range(ROW_CAP):
        source = matrix.at[pl.ds(pl.multiple_of(row_at[s] * BLK, BLK), BLK), pl.ds(0, BLK)]
        target = panel_out.at[pl.ds(s * BLK, BLK)]
        copies.append(pltpu.make_async_copy(source, target, sems.at[COL_CAP + s]))
    for copy in copies:
        copy.start()
    for copy in copies:
        copy.wait()
    own = (pcol == 1).astype(jnp.int32)
    for s in range(ROW_CAP):
        stored = (count > s) & (row_pattern[own, prow * row_blocks + row_at[s]] > 0)

        @pl.when(jnp.logical_not(stored))
        def _(s=s):
            panel_out[pl.ds(s * BLK, BLK), :] = jnp.zeros((BLK, BLK), jnp.bfloat16)


def pack(here, row_pattern, col_pattern, matrix):
    smem = pl.BlockSpec(memory_space=pltpu.SMEM)
    vmem = pl.BlockSpec(memory_space=pltpu.VMEM)
    return pl.pallas_call(
        pack_kernel,
        in_specs=[smem, smem, smem, pl.BlockSpec(memory_space=pl.ANY)],
        out_specs=[vmem] * 3,
        out_shape=[
            vmem_shape(BLK, BLK),
            vmem_shape((COL_CAP - 1) * BLK, BLK),
            vmem_shape(ROW_CAP * BLK, BLK),
        ],
        scratch_shapes=[pltpu.SemaphoreType.DMA((COL_CAP + ROW_CAP,))],
        name="pack",
    )(here, row_pattern, col_pattern, matrix)


def in_vmem(*values):
    return [pltpu.with_memory_space_constraint(v, pltpu.VMEM) for v in values]


def vmem_shape(*shape):
    return pltpu.VMEM(shape, jnp.bfloat16)


def halves(value):
    high = value.astype(jnp.bfloat16)
    return high, (value - high.astype(jnp.float32)).astype(jnp.bfloat16)


def dot(a, b):
    return jnp.dot(a, b, preferred_element_type=jnp.float32)


def panels_kernel(here, row_pattern, mine, other, lower_0, lower_1):
    prow, core_0 = here[0], here[1] % 2 == 0
    row_blocks = row_pattern.shape[1] // (X * Y)

    def of_core(core, block):
        at = pl.ds(block * BLK, BLK)
        own = core_0 if core == 0 else jnp.logical_not(core_0)
        return jnp.where(own, mine[at, :], other[at, :])

    i = lax.broadcasted_iota(jnp.int32, (BLK, BLK), 0)
    j = lax.broadcasted_iota(jnp.int32, (BLK, BLK), 1)
    diagonal = i == j
    powers, sums, scales = [], [], []
    for n in range(2):
        p = of_core(n, n).astype(jnp.float32)
        d = jnp.where(diagonal, p, 0.0)
        by_row = jnp.sum(d, axis=1, keepdims=True)
        scales.append(1.0 / jnp.sum(d, axis=0, keepdims=True))
        r = jnp.where(diagonal, 0.0, -p / by_row)
        powers.append(r)
        sums.append(jnp.where(diagonal, 1.0, r))
    for step in range(8):
        for n in range(2):
            high, low = halves(powers[n])
            if step > 0:
                sum_high, sum_low = halves(sums[n])
                sums[n] = sums[n] + (
                    dot(high, sum_high) + (dot(high, sum_low) + dot(low, sum_high))
                )
            if step < 7:
                powers[n] = dot(high, high) + (dot(high, low) + dot(low, high))
    rows = [row_pattern[1, prow * row_blocks + b] > 0 for b in range(row_blocks)]
    _, row_at, _ = slots(rows, ROW_CAP)
    inverses = [halves(sums[n] * scales[n]) for n in range(2)]
    upper_01 = of_core(1, 0)
    for s in range(ROW_CAP):
        at = pl.ds(s * BLK, BLK)
        panel = of_core(0, 2 + s)
        high, low = inverses[0]
        lower = dot(panel, high) + dot(panel, low)
        done = (prow == 0) & (row_at[s] == 0)
        lower = jnp.where(done, 0.0, lower).astype(jnp.bfloat16)
        lower_0[at, :] = lower
        panel = of_core(1, 2 + s).astype(jnp.float32) - dot(lower, upper_01)
        panel = panel.astype(jnp.bfloat16)
        high, low = inverses[1]
        lower = dot(panel, high) + dot(panel, low)
        done = (prow <= 1) & (row_at[s] == 0)
        lower_1[at, :] = jnp.where(done, 0.0, lower).astype(jnp.bfloat16)


def panels(here, row_pattern, mine, other):
    smem = pl.BlockSpec(memory_space=pltpu.SMEM)
    vmem = pl.BlockSpec(memory_space=pltpu.VMEM)
    shape = vmem_shape(ROW_CAP * BLK, BLK)
    return pl.pallas_call(
        panels_kernel,
        in_specs=[smem, smem] + [vmem] * 2,
        out_specs=[vmem] * 2,
        out_shape=[shape, shape],
        cost_estimate=pl.CostEstimate(
            flops=120 * BLK**3, bytes_accessed=24 * BLK * BLK, transcendentals=0
        ),
        name="panels",
    )(here, row_pattern, *in_vmem(mine, other))


def update_kernel(
    here, row_pattern, col_pattern, source, lower_0, lower_1,
    first_held, first_came, rest_held, up_came, down_came, out, upper,
):
    prow, pcol = here[0], here[1]
    i = pl.program_id(0)
    row_blocks = pl.num_programs(0)
    col_blocks = source.shape[1] // BLK

    @pl.when(i == 0)
    def _():
        even = prow % 2 == 0
        for s in range(COL_CAP):
            rest = pl.ds((s - 1) * BLK, BLK)
            held = first_held[...] if s == 0 else rest_held[rest, :]
            came = (
                first_came[...]
                if s == 0
                else up_came[...]
                if s == COL_CAP - 1
                else down_came[rest, :]
            )
            upper[0, pl.ds(s * BLK, BLK), :] = jnp.where(even, held, came)
            upper[1, pl.ds(s * BLK, BLK), :] = jnp.where(even, came, held)

    row = prow * row_blocks + i
    slot = jnp.int32(0)
    for b in range(2):
        slot = slot + ((i > b) & (row_pattern[1, prow * row_blocks + b] > 0)).astype(jnp.int32)
    rows = pl.ds(pl.multiple_of(jnp.minimum(slot, ROW_CAP - 1) * BLK, BLK), BLK)
    stored = [row_pattern[k, row] > 0 for k in range(2)]
    first = i == 0
    done = [first & (prow == 0), first & (prow <= 1)]
    lower = [lower_0, lower_1]
    flags = [[col_pattern[k, pcol * col_blocks + j] > 0 for j in range(col_blocks)] for k in (0, 1)]
    col_slot = [slots(f, COL_CAP)[0] for f in flags]
    for j in range(col_blocks):
        columns = pl.ds(j * BLK, BLK)
        dropped = jnp.bool_(False)
        used = []
        for k in range(2):
            dropped = dropped | (first & (prow == k) & jnp.logical_not(flags[k][j]))
            use = stored[k] & jnp.logical_not(done[k]) & flags[k][j]
            if j == 0:
                dropped = dropped | ((pcol == k) & jnp.logical_not(stored[k]))
                use = use & (pcol > k)
            used.append(use)
        other = used[0] | used[1]

        def product(k, j=j):
            at = pl.ds(pl.multiple_of(col_slot[k][j] * BLK, BLK), BLK)
            return dot(lower[k][rows, :], upper[k, at, :])

        def kept(columns=columns, dropped=dropped):
            value = source[:, columns]
            return jnp.where(dropped, jnp.zeros_like(value), value)

        def reduced(value, k, j=j):
            return (value.astype(jnp.float32) - product(k, j)).astype(jnp.bfloat16)

        @pl.when(jnp.logical_not(other))
        def _(columns=columns, kept=kept):
            out[:, columns] = kept()

        @pl.when(used[0] & jnp.logical_not(used[1]))
        def _(columns=columns, kept=kept, reduced=reduced):
            out[:, columns] = reduced(kept(), 0)

        @pl.when(used[1] & jnp.logical_not(used[0]))
        def _(columns=columns, kept=kept, reduced=reduced):
            out[:, columns] = reduced(kept(), 1)

        @pl.when(used[0] & used[1])
        def _(columns=columns, kept=kept, reduced=reduced):
            out[:, columns] = reduced(reduced(kept(), 0), 1)

        if j == 0:
            for k in range(2):

                @pl.when((pcol == k) & jnp.logical_not(done[k]))
                def _(k=k, columns=columns):
                    value = lower[k][rows, :]
                    out[:, columns] = jnp.where(stored[k], value, jnp.zeros_like(value))


def update(here, row_pattern, col_pattern, matrix, *blocks):
    row_blocks = matrix.shape[0] // BLK
    breadth = matrix.shape[1]
    smem = pl.BlockSpec(memory_space=pltpu.SMEM)
    vmem = pl.BlockSpec(memory_space=pltpu.VMEM)
    strip = pl.BlockSpec((BLK, breadth), lambda i: (i, 0))
    return pl.pallas_call(
        update_kernel,
        grid=(row_blocks,),
        in_specs=[smem] * 3 + [strip] + [vmem] * 7,
        out_specs=strip,
        out_shape=jax.ShapeDtypeStruct(matrix.shape, matrix.dtype),
        scratch_shapes=[pltpu.VMEM((2, COL_CAP * BLK, BLK), jnp.bfloat16)],
        name="update",
    )(here, row_pattern, col_pattern, matrix, *in_vmem(*blocks))


def shards(matrix, row_pattern, col_pattern):
    prow = lax.axis_index(PROW).astype(jnp.int32)
    pcol = lax.axis_index("pcol").astype(jnp.int32)
    even = prow % 2 == 0
    here = jnp.where(jnp.arange(2) == 0, prow, pcol)
    first, rest, panel = pack(here, row_pattern, col_pattern, matrix)
    zero = jnp.zeros((), jnp.bfloat16)

    def tree(value, root, levels):
        held = jnp.where(root, value, zero)
        for level, letter in zip(levels, "abc"):
            source = value if letter == "a" else held
            for pairs in level:
                held = held + send(source, pairs)
        return held

    first_held = tree(first, prow <= 1, SPREAD)
    first_came = send(first_held, UP)
    rest_held = tree(rest, prow <= 1, SPREAD)
    down_came = send(rest_held[: 2 * BLK], DOWN)
    up_came = send(rest_held[2 * BLK :], UP)
    panel = tree(panel, pcol <= 1, [LINE_1, LINE_2])
    pivots = jnp.concatenate(
        [
            jnp.where(even, first_held, first_came),
            jnp.where(even, first_came, first_held),
        ],
        axis=0,
    )
    pivots = tree(pivots, pcol <= 1, [LINE_1, LINE_2])
    mine = jnp.concatenate([pivots, panel], axis=0)
    other = send(mine, SWAP)
    lower_0, lower_1 = panels(here, row_pattern, mine, other)
    return update(
        here, row_pattern, col_pattern, matrix, lower_0, lower_1,
        first_held, first_came, rest_held, up_came, down_came,
    )


def solution(mesh):
    torus = Mesh(mesh.devices.reshape(X, Y, mesh.shape["pcol"]), AXES)
    placed = (P(PROW, "pcol"), P(), P())
    return jax.shard_map(
        shards, mesh=torus, in_specs=placed, out_specs=P(PROW, "pcol"), check_vma=False
    )
```

```python
import jax
import jax.numpy as jnp
from jax import lax
from jax.experimental import pallas as pl
from jax.experimental.pallas import tpu as pltpu
from jax.sharding import Mesh
from jax.sharding import PartitionSpec as P


BLK = 256
X, Y, Z = 4, 8, 8
AXES = ("prow_0", "prow_1", "pcol")
PROW = ("prow_0", "prow_1")
ROW_CAP, COL_CAP = 2, 4


def device(x, y, z, core):
    return ((x % X) * Y + y % Y) * (2 * Z) + (z % Z) * 2 + core


def plane_pairs(pairs):
    out = []
    for (xs, ys), (xt, yt) in pairs:
        for z in range(Z):
            for core in range(2):
                out.append((device(xs, ys, z, core), device(xt, yt, z, core)))
                out.append((device(xs, 1 - ys, z, core), device(xt, 1 - yt, z, core)))
    return out


def line_pairs(pairs):
    return [
        (device(x, y, s, core), device(x, y, t, core))
        for s, t in pairs
        for x in range(X)
        for y in range(Y)
        for core in range(2)
    ]


SPREAD = [
    [plane_pairs([((0, 0), h)]) for h in ((2, 6), (1, 0), (3, 0))],
    [plane_pairs([((0, 0), (0, 6)), ((1, 0), (1, 6)), ((3, 0), (3, 6)), ((2, 6), (2, 0))])],
    [plane_pairs([((x, 0), (x, 2)) for x in range(X)] + [((x, 6), (x, 4)) for x in range(X)])],
]
UP = [
    (device(x, y, z, c), device(x, y + 1, z, c))
    for x in range(X) for y in range(Y) for z in range(Z) for c in range(2)
]
DOWN = [(t, s) for s, t in UP]
LINE_1 = [line_pairs([(0, 3)]), line_pairs([(0, 5)])]
LINE_2 = [line_pairs([(0, 1), (3, 4), (5, 6)]), line_pairs([(0, 7), (3, 2)])]
SWAP = [
    (device(x, y, z, c), device(x, y, z, 1 - c))
    for x in range(X) for y in range(Y) for z in range(Z) for c in range(2)
]


def send(value, pairs):
    return lax.ppermute(value, AXES, pairs)


def slots(flags, capacity):
    count = jnp.int32(0)
    slot_of = []
    where = [jnp.int32(0)] * capacity
    for position, flag in enumerate(flags):
        one = flag.astype(jnp.int32)
        slot_of.append(jnp.minimum(count, capacity - 1))
        where = [
            jnp.where(flag & (count == s), jnp.int32(position), w) for s, w in enumerate(where)
        ]
        count = count + one
    return slot_of, where, count


def pack_kernel(here, row_pattern, col_pattern, matrix, first_out, rest_out, panel_out, sems):
    prow, pcol = here[0], here[1]
    row_blocks, col_blocks = matrix.shape[0] // BLK, matrix.shape[1] // BLK
    k = (prow == 1).astype(jnp.int32)
    cols = [col_pattern[k, pcol * col_blocks + j] > 0 for j in range(col_blocks)]
    _, col_at, _ = slots(cols, COL_CAP)
    copies = []
    for s in range(COL_CAP):
        source = matrix.at[pl.ds(0, BLK), pl.ds(pl.multiple_of(col_at[s] * BLK, BLK), BLK)]
        target = first_out if s == 0 else rest_out.at[pl.ds((s - 1) * BLK, BLK)]
        copies.append(pltpu.make_async_copy(source, target, sems.at[s]))
    rows = [row_pattern[1, prow * row_blocks + i] > 0 for i in range(row_blocks)]
    _, row_at, count = slots(rows, ROW_CAP)
    for s in range(ROW_CAP):
        source = matrix.at[pl.ds(pl.multiple_of(row_at[s] * BLK, BLK), BLK), pl.ds(0, BLK)]
        target = panel_out.at[pl.ds(s * BLK, BLK)]
        copies.append(pltpu.make_async_copy(source, target, sems.at[COL_CAP + s]))
    for copy in copies:
        copy.start()
    for copy in copies:
        copy.wait()
    own = (pcol == 1).astype(jnp.int32)
    for s in range(ROW_CAP):
        stored = (count > s) & (row_pattern[own, prow * row_blocks + row_at[s]] > 0)

        @pl.when(jnp.logical_not(stored))
        def _(s=s):
            panel_out[pl.ds(s * BLK, BLK), :] = jnp.zeros((BLK, BLK), jnp.bfloat16)


def pack(here, row_pattern, col_pattern, matrix):
    smem = pl.BlockSpec(memory_space=pltpu.SMEM)
    vmem = pl.BlockSpec(memory_space=pltpu.VMEM)
    return pl.pallas_call(
        pack_kernel,
        in_specs=[smem, smem, smem, pl.BlockSpec(memory_space=pl.ANY)],
        out_specs=[vmem] * 3,
        out_shape=[
            vmem_shape(BLK, BLK),
            vmem_shape((COL_CAP - 1) * BLK, BLK),
            vmem_shape(ROW_CAP * BLK, BLK),
        ],
        scratch_shapes=[pltpu.SemaphoreType.DMA((COL_CAP + ROW_CAP,))],
        name="pack",
    )(here, row_pattern, col_pattern, matrix)


def in_vmem(*values):
    return [pltpu.with_memory_space_constraint(v, pltpu.VMEM) for v in values]


def vmem_shape(*shape):
    return pltpu.VMEM(shape, jnp.bfloat16)


def halves(value):
    high = value.astype(jnp.bfloat16)
    return high, (value - high.astype(jnp.float32)).astype(jnp.bfloat16)


def dot(a, b):
    return jnp.dot(a, b, preferred_element_type=jnp.float32)


def panels_kernel(here, row_pattern, mine, other, lower_0, lower_1):
    prow, core_0 = here[0], here[1] % 2 == 0
    row_blocks = row_pattern.shape[1] // (X * Y)

    def of_core(core, block):
        at = pl.ds(block * BLK, BLK)
        own = core_0 if core == 0 else jnp.logical_not(core_0)
        return jnp.where(own, mine[at, :], other[at, :])

    i = lax.broadcasted_iota(jnp.int32, (BLK, BLK), 0)
    j = lax.broadcasted_iota(jnp.int32, (BLK, BLK), 1)
    diagonal = i == j
    powers, sums, scales = [], [], []
    for n in range(2):
        p = of_core(n, n).astype(jnp.float32)
        d = jnp.where(diagonal, p, 0.0)
        by_row = jnp.sum(d, axis=1, keepdims=True)
        scales.append(1.0 / jnp.sum(d, axis=0, keepdims=True))
        r = jnp.where(diagonal, 0.0, -p / by_row)
        powers.append(r)
        sums.append(jnp.where(diagonal, 1.0, r))
    for step in range(8):
        for n in range(2):
            if step >= 5:
                high = powers[n].astype(jnp.bfloat16)
                sums[n] = sums[n] + dot(high, sums[n].astype(jnp.bfloat16))
                if step < 7:
                    powers[n] = dot(high, high)
                continue
            high, low = halves(powers[n])
            if step > 0:
                sum_high, sum_low = halves(sums[n])
                sums[n] = sums[n] + (
                    dot(high, sum_high) + (dot(high, sum_low) + dot(low, sum_high))
                )
            if step < 7:
                powers[n] = dot(high, high) + (dot(high, low) + dot(low, high))
    rows = [row_pattern[1, prow * row_blocks + b] > 0 for b in range(row_blocks)]
    _, row_at, _ = slots(rows, ROW_CAP)
    inverses = [halves(sums[n] * scales[n]) for n in range(2)]
    upper_01 = of_core(1, 0)
    for s in range(ROW_CAP):
        at = pl.ds(s * BLK, BLK)
        panel = of_core(0, 2 + s)
        high, low = inverses[0]
        lower = dot(panel, high) + dot(panel, low)
        done = (prow == 0) & (row_at[s] == 0)
        lower = jnp.where(done, 0.0, lower).astype(jnp.bfloat16)
        lower_0[at, :] = lower
        panel = of_core(1, 2 + s).astype(jnp.float32) - dot(lower, upper_01)
        panel = panel.astype(jnp.bfloat16)
        high, low = inverses[1]
        lower = dot(panel, high) + dot(panel, low)
        done = (prow <= 1) & (row_at[s] == 0)
        lower_1[at, :] = jnp.where(done, 0.0, lower).astype(jnp.bfloat16)


def panels(here, row_pattern, mine, other):
    smem = pl.BlockSpec(memory_space=pltpu.SMEM)
    vmem = pl.BlockSpec(memory_space=pltpu.VMEM)
    shape = vmem_shape(ROW_CAP * BLK, BLK)
    return pl.pallas_call(
        panels_kernel,
        in_specs=[smem, smem] + [vmem] * 2,
        out_specs=[vmem] * 2,
        out_shape=[shape, shape],
        cost_estimate=pl.CostEstimate(
            flops=120 * BLK**3, bytes_accessed=24 * BLK * BLK, transcendentals=0
        ),
        name="panels",
    )(here, row_pattern, *in_vmem(mine, other))


def update_kernel(
    here, row_pattern, col_pattern, source, lower_0, lower_1,
    first_held, rest_held, up_came, down_came, out, upper,
):
    prow, pcol = here[0], here[1]
    i = pl.program_id(0)
    row_blocks = pl.num_programs(0)
    col_blocks = source.shape[1] // BLK

    @pl.when(i == 0)
    def _():
        even = prow % 2 == 0
        for s in range(COL_CAP):
            rest = pl.ds((s - 1) * BLK, BLK)
            held = first_held[...] if s == 0 else rest_held[rest, :]
            if s == 0:
                came = up_came[pl.ds(0, BLK), :]
            elif s == COL_CAP - 1:
                came = up_came[pl.ds(BLK, BLK), :]
            else:
                came = down_came[rest, :]
            upper[0, pl.ds(s * BLK, BLK), :] = jnp.where(even, held, came)
            upper[1, pl.ds(s * BLK, BLK), :] = jnp.where(even, came, held)

    row = prow * row_blocks + i
    slot = jnp.int32(0)
    for b in range(2):
        slot = slot + ((i > b) & (row_pattern[1, prow * row_blocks + b] > 0)).astype(jnp.int32)
    rows = pl.ds(pl.multiple_of(jnp.minimum(slot, ROW_CAP - 1) * BLK, BLK), BLK)
    stored = [row_pattern[k, row] > 0 for k in range(2)]
    first = i == 0
    done = [first & (prow == 0), first & (prow <= 1)]
    lower = [lower_0, lower_1]
    flags = [[col_pattern[k, pcol * col_blocks + j] > 0 for j in range(col_blocks)] for k in (0, 1)]
    col_slot = [slots(f, COL_CAP)[0] for f in flags]
    for j in range(col_blocks):
        columns = pl.ds(j * BLK, BLK)
        dropped = jnp.bool_(False)
        used = []
        for k in range(2):
            dropped = dropped | (first & (prow == k) & jnp.logical_not(flags[k][j]))
            use = stored[k] & jnp.logical_not(done[k]) & flags[k][j]
            if j == 0:
                dropped = dropped | ((pcol == k) & jnp.logical_not(stored[k]))
                use = use & (pcol > k)
            used.append(use)
        other = used[0] | used[1]

        def product(k, j=j):
            at = pl.ds(pl.multiple_of(col_slot[k][j] * BLK, BLK), BLK)
            return dot(lower[k][rows, :], upper[k, at, :])

        def kept(columns=columns, dropped=dropped):
            value = source[:, columns]
            return jnp.where(dropped, jnp.zeros_like(value), value)

        def reduced(value, k, j=j):
            return (value.astype(jnp.float32) - product(k, j)).astype(jnp.bfloat16)

        @pl.when(jnp.logical_not(other))
        def _(columns=columns, kept=kept):
            out[:, columns] = kept()

        @pl.when(used[0] & jnp.logical_not(used[1]))
        def _(columns=columns, kept=kept, reduced=reduced):
            out[:, columns] = reduced(kept(), 0)

        @pl.when(used[1] & jnp.logical_not(used[0]))
        def _(columns=columns, kept=kept, reduced=reduced):
            out[:, columns] = reduced(kept(), 1)

        @pl.when(used[0] & used[1])
        def _(columns=columns, kept=kept, reduced=reduced):
            out[:, columns] = reduced(reduced(kept(), 0), 1)

        if j == 0:
            for k in range(2):

                @pl.when((pcol == k) & jnp.logical_not(done[k]))
                def _(k=k, columns=columns):
                    value = lower[k][rows, :]
                    out[:, columns] = jnp.where(stored[k], value, jnp.zeros_like(value))


def update(here, row_pattern, col_pattern, matrix, *blocks):
    row_blocks = matrix.shape[0] // BLK
    breadth = matrix.shape[1]
    smem = pl.BlockSpec(memory_space=pltpu.SMEM)
    vmem = pl.BlockSpec(memory_space=pltpu.VMEM)
    strip = pl.BlockSpec((BLK, breadth), lambda i: (i, 0))
    return pl.pallas_call(
        update_kernel,
        grid=(row_blocks,),
        in_specs=[smem] * 3 + [strip] + [vmem] * 6,
        out_specs=strip,
        out_shape=jax.ShapeDtypeStruct(matrix.shape, matrix.dtype),
        scratch_shapes=[pltpu.VMEM((2, COL_CAP * BLK, BLK), jnp.bfloat16)],
        name="update",
    )(here, row_pattern, col_pattern, matrix, *in_vmem(*blocks))


def shards(matrix, row_pattern, col_pattern):
    prow = lax.axis_index(PROW).astype(jnp.int32)
    pcol = lax.axis_index("pcol").astype(jnp.int32)
    even = prow % 2 == 0
    here = jnp.where(jnp.arange(2) == 0, prow, pcol)
    first, rest, panel = pack(here, row_pattern, col_pattern, matrix)
    zero = jnp.zeros((), jnp.bfloat16)

    def tree(value, root, levels):
        held = jnp.where(root, value, zero)
        for level, letter in zip(levels, "abc"):
            source = value if letter == "a" else held
            for pairs in level:
                held = held + send(source, pairs)
        return held

    first_held = tree(first, prow <= 1, SPREAD)
    rest_held = tree(rest, prow <= 1, SPREAD)
    down_came = send(rest_held[: 2 * BLK], DOWN)
    up_came = send(jnp.concatenate([first_held, rest_held[2 * BLK :]], axis=0), UP)
    panel = tree(panel, pcol <= 1, [LINE_1, LINE_2])
    pivot_held = tree(first_held, pcol <= 1, [LINE_1, LINE_2])
    pivot_came = send(pivot_held, UP)
    mine = jnp.concatenate(
        [jnp.where(even, pivot_held, pivot_came), jnp.where(even, pivot_came, pivot_held), panel],
        axis=0,
    )
    other = send(mine, SWAP)
    lower_0, lower_1 = panels(here, row_pattern, mine, other)
    return update(
        here, row_pattern, col_pattern, matrix, lower_0, lower_1,
        first_held, rest_held, up_came, down_came,
    )


def solution(mesh):
    torus = Mesh(mesh.devices.reshape(X, Y, mesh.shape["pcol"]), AXES)
    placed = (P(PROW, "pcol"), P(), P())
    return jax.shard_map(
        shards, mesh=torus, in_specs=placed, out_specs=P(PROW, "pcol"), check_vma=False
    )
```

```python
import jax
import jax.numpy as jnp
from jax import lax
from jax.experimental import pallas as pl
from jax.experimental.pallas import tpu as pltpu
from jax.sharding import Mesh
from jax.sharding import PartitionSpec as P


BLK = 256
X, Y, Z = 4, 8, 8
AXES = ("prow_0", "prow_1", "pcol")
PROW = ("prow_0", "prow_1")
ROW_CAP, COL_CAP = 2, 4


def device(x, y, z, core):
    return ((x % X) * Y + y % Y) * (2 * Z) + (z % Z) * 2 + core


def plane_pairs(pairs):
    out = []
    for (xs, ys), (xt, yt) in pairs:
        for z in range(Z):
            for core in range(2):
                out.append((device(xs, ys, z, core), device(xt, yt, z, core)))
                out.append((device(xs, 1 - ys, z, core), device(xt, 1 - yt, z, core)))
    return out


def line_pairs(pairs):
    return [
        (device(x, y, s, core), device(x, y, t, core))
        for s, t in pairs
        for x in range(X)
        for y in range(Y)
        for core in range(2)
    ]


SPREAD = [
    [plane_pairs([((0, 0), h)]) for h in ((2, 6), (1, 0), (3, 0))],
    [plane_pairs([((0, 0), (0, 6)), ((1, 0), (1, 6)), ((3, 0), (3, 6)), ((2, 6), (2, 0))])],
    [plane_pairs([((x, 0), (x, 2)) for x in range(X)] + [((x, 6), (x, 4)) for x in range(X)])],
]
SPREAD_REST = [
    [plane_pairs([((0, 0), (x, 0))]) for x in (2, 1, 3)],
    [plane_pairs([((x, 0), (x, 6)) for x in range(X)])],
    SPREAD[2],
]
UP = [
    (device(x, y, z, c), device(x, y + 1, z, c))
    for x in range(X) for y in range(Y) for z in range(Z) for c in range(2)
]
DOWN = [(t, s) for s, t in UP]
LINE_1 = [line_pairs([(0, 3)]), line_pairs([(0, 5)])]
LINE_2 = [line_pairs([(0, 1), (3, 4), (5, 6)]), line_pairs([(0, 7), (3, 2)])]
SWAP = [
    (device(x, y, z, c), device(x, y, z, 1 - c))
    for x in range(X) for y in range(Y) for z in range(Z) for c in range(2)
]


def send(value, pairs):
    return lax.ppermute(value, AXES, pairs)


def slots(flags, capacity):
    count = jnp.int32(0)
    slot_of = []
    where = [jnp.int32(0)] * capacity
    for position, flag in enumerate(flags):
        one = flag.astype(jnp.int32)
        slot_of.append(jnp.minimum(count, capacity - 1))
        where = [
            jnp.where(flag & (count == s), jnp.int32(position), w) for s, w in enumerate(where)
        ]
        count = count + one
    return slot_of, where, count


def pack_kernel(here, row_pattern, col_pattern, matrix, first_out, rest_out, panel_out, sems):
    prow, pcol = here[0], here[1]
    row_blocks, col_blocks = matrix.shape[0] // BLK, matrix.shape[1] // BLK
    k = (prow == 1).astype(jnp.int32)
    cols = [col_pattern[k, pcol * col_blocks + j] > 0 for j in range(col_blocks)]
    _, col_at, _ = slots(cols, COL_CAP)
    copies = []
    for s in range(COL_CAP):
        source = matrix.at[pl.ds(0, BLK), pl.ds(pl.multiple_of(col_at[s] * BLK, BLK), BLK)]
        target = first_out if s == 0 else rest_out.at[pl.ds((s - 1) * BLK, BLK)]
        copies.append(pltpu.make_async_copy(source, target, sems.at[s]))
    rows = [row_pattern[1, prow * row_blocks + i] > 0 for i in range(row_blocks)]
    _, row_at, count = slots(rows, ROW_CAP)
    for s in range(ROW_CAP):
        source = matrix.at[pl.ds(pl.multiple_of(row_at[s] * BLK, BLK), BLK), pl.ds(0, BLK)]
        target = panel_out.at[pl.ds(s * BLK, BLK)]
        copies.append(pltpu.make_async_copy(source, target, sems.at[COL_CAP + s]))
    for copy in copies:
        copy.start()
    for copy in copies:
        copy.wait()
    own = (pcol == 1).astype(jnp.int32)
    for s in range(ROW_CAP):
        stored = (count > s) & (row_pattern[own, prow * row_blocks + row_at[s]] > 0)

        @pl.when(jnp.logical_not(stored))
        def _(s=s):
            panel_out[pl.ds(s * BLK, BLK), :] = jnp.zeros((BLK, BLK), jnp.bfloat16)


def pack(here, row_pattern, col_pattern, matrix):
    smem = pl.BlockSpec(memory_space=pltpu.SMEM)
    vmem = pl.BlockSpec(memory_space=pltpu.VMEM)
    return pl.pallas_call(
        pack_kernel,
        in_specs=[smem, smem, smem, pl.BlockSpec(memory_space=pl.ANY)],
        out_specs=[vmem] * 3,
        out_shape=[
            vmem_shape(BLK, BLK),
            vmem_shape((COL_CAP - 1) * BLK, BLK),
            vmem_shape(ROW_CAP * BLK, BLK),
        ],
        scratch_shapes=[pltpu.SemaphoreType.DMA((COL_CAP + ROW_CAP,))],
        name="pack",
    )(here, row_pattern, col_pattern, matrix)


def in_vmem(*values):
    return [pltpu.with_memory_space_constraint(v, pltpu.VMEM) for v in values]


def vmem_shape(*shape):
    return pltpu.VMEM(shape, jnp.bfloat16)


def halves(value):
    high = value.astype(jnp.bfloat16)
    return high, (value - high.astype(jnp.float32)).astype(jnp.bfloat16)


def dot(a, b):
    return jnp.dot(a, b, preferred_element_type=jnp.float32)


def panels_kernel(here, row_pattern, mine, other, lower_0, lower_1):
    prow, core_0 = here[0], here[1] % 2 == 0
    row_blocks = row_pattern.shape[1] // (X * Y)

    def of_core(core, block):
        at = pl.ds(block * BLK, BLK)
        own = core_0 if core == 0 else jnp.logical_not(core_0)
        return jnp.where(own, mine[at, :], other[at, :])

    i = lax.broadcasted_iota(jnp.int32, (BLK, BLK), 0)
    j = lax.broadcasted_iota(jnp.int32, (BLK, BLK), 1)
    diagonal = i == j
    powers, sums, scales = [], [], []
    for n in range(2):
        p = of_core(n, n).astype(jnp.float32)
        d = jnp.where(diagonal, p, 0.0)
        by_row = jnp.sum(d, axis=1, keepdims=True)
        scales.append(1.0 / jnp.sum(d, axis=0, keepdims=True))
        r = jnp.where(diagonal, 0.0, -p / by_row)
        powers.append(r)
        sums.append(jnp.where(diagonal, 1.0, r))
    for step in range(8):
        for n in range(2):
            if step >= 5:
                high = powers[n].astype(jnp.bfloat16)
                sums[n] = sums[n] + dot(high, sums[n].astype(jnp.bfloat16))
                if step < 7:
                    powers[n] = dot(high, high)
                continue
            high, low = halves(powers[n])
            if step > 0:
                sum_high, sum_low = halves(sums[n])
                sums[n] = sums[n] + (
                    dot(high, sum_high) + (dot(high, sum_low) + dot(low, sum_high))
                )
            if step < 7:
                powers[n] = dot(high, high) + (dot(high, low) + dot(low, high))
    rows = [row_pattern[1, prow * row_blocks + b] > 0 for b in range(row_blocks)]
    _, row_at, _ = slots(rows, ROW_CAP)
    inverses = [halves(sums[n] * scales[n]) for n in range(2)]
    upper_01 = of_core(1, 0)
    for s in range(ROW_CAP):
        at = pl.ds(s * BLK, BLK)
        panel = of_core(0, 2 + s)
        high, low = inverses[0]
        lower = dot(panel, high) + dot(panel, low)
        done = (prow == 0) & (row_at[s] == 0)
        lower = jnp.where(done, 0.0, lower).astype(jnp.bfloat16)
        lower_0[at, :] = lower
        panel = of_core(1, 2 + s).astype(jnp.float32) - dot(lower, upper_01)
        panel = panel.astype(jnp.bfloat16)
        high, low = inverses[1]
        lower = dot(panel, high) + dot(panel, low)
        done = (prow <= 1) & (row_at[s] == 0)
        lower_1[at, :] = jnp.where(done, 0.0, lower).astype(jnp.bfloat16)


def panels(here, row_pattern, mine, other):
    smem = pl.BlockSpec(memory_space=pltpu.SMEM)
    vmem = pl.BlockSpec(memory_space=pltpu.VMEM)
    shape = vmem_shape(ROW_CAP * BLK, BLK)
    return pl.pallas_call(
        panels_kernel,
        in_specs=[smem, smem] + [vmem] * 2,
        out_specs=[vmem] * 2,
        out_shape=[shape, shape],
        cost_estimate=pl.CostEstimate(
            flops=120 * BLK**3, bytes_accessed=24 * BLK * BLK, transcendentals=0
        ),
        name="panels",
    )(here, row_pattern, *in_vmem(mine, other))


def update_kernel(
    here, row_pattern, col_pattern, source, lower_0, lower_1,
    first_held, rest_held, up_came, down_came, out, upper,
):
    prow, pcol = here[0], here[1]
    i = pl.program_id(0)
    row_blocks = pl.num_programs(0)
    col_blocks = source.shape[1] // BLK

    @pl.when(i == 0)
    def _():
        even = prow % 2 == 0
        for s in range(COL_CAP):
            rest = pl.ds((s - 1) * BLK, BLK)
            held = first_held[...] if s == 0 else rest_held[rest, :]
            if s == 0:
                came = up_came[pl.ds(0, BLK), :]
            elif s == COL_CAP - 1:
                came = up_came[pl.ds(BLK, BLK), :]
            else:
                came = down_came[rest, :]
            upper[0, pl.ds(s * BLK, BLK), :] = jnp.where(even, held, came)
            upper[1, pl.ds(s * BLK, BLK), :] = jnp.where(even, came, held)

    row = prow * row_blocks + i
    slot = jnp.int32(0)
    for b in range(2):
        slot = slot + ((i > b) & (row_pattern[1, prow * row_blocks + b] > 0)).astype(jnp.int32)
    rows = pl.ds(pl.multiple_of(jnp.minimum(slot, ROW_CAP - 1) * BLK, BLK), BLK)
    stored = [row_pattern[k, row] > 0 for k in range(2)]
    first = i == 0
    done = [first & (prow == 0), first & (prow <= 1)]
    lower = [lower_0, lower_1]
    flags = [[col_pattern[k, pcol * col_blocks + j] > 0 for j in range(col_blocks)] for k in (0, 1)]
    col_slot = [slots(f, COL_CAP)[0] for f in flags]
    for j in range(col_blocks):
        columns = pl.ds(j * BLK, BLK)
        dropped = jnp.bool_(False)
        used = []
        for k in range(2):
            dropped = dropped | (first & (prow == k) & jnp.logical_not(flags[k][j]))
            use = stored[k] & jnp.logical_not(done[k]) & flags[k][j]
            if j == 0:
                dropped = dropped | ((pcol == k) & jnp.logical_not(stored[k]))
                use = use & (pcol > k)
            used.append(use)
        other = used[0] | used[1]

        def product(k, j=j):
            at = pl.ds(pl.multiple_of(col_slot[k][j] * BLK, BLK), BLK)
            return dot(lower[k][rows, :], upper[k, at, :])

        def kept(columns=columns, dropped=dropped):
            value = source[:, columns]
            return jnp.where(dropped, jnp.zeros_like(value), value)

        def reduced(value, k, j=j):
            return (value.astype(jnp.float32) - product(k, j)).astype(jnp.bfloat16)

        @pl.when(jnp.logical_not(other))
        def _(columns=columns, kept=kept):
            out[:, columns] = kept()

        @pl.when(used[0] & jnp.logical_not(used[1]))
        def _(columns=columns, kept=kept, reduced=reduced):
            out[:, columns] = reduced(kept(), 0)

        @pl.when(used[1] & jnp.logical_not(used[0]))
        def _(columns=columns, kept=kept, reduced=reduced):
            out[:, columns] = reduced(kept(), 1)

        @pl.when(used[0] & used[1])
        def _(columns=columns, kept=kept, reduced=reduced):
            out[:, columns] = reduced(reduced(kept(), 0), 1)

        if j == 0:
            for k in range(2):

                @pl.when((pcol == k) & jnp.logical_not(done[k]))
                def _(k=k, columns=columns):
                    value = lower[k][rows, :]
                    out[:, columns] = jnp.where(stored[k], value, jnp.zeros_like(value))


def update(here, row_pattern, col_pattern, matrix, *blocks):
    row_blocks = matrix.shape[0] // BLK
    breadth = matrix.shape[1]
    smem = pl.BlockSpec(memory_space=pltpu.SMEM)
    vmem = pl.BlockSpec(memory_space=pltpu.VMEM)
    strip = pl.BlockSpec((BLK, breadth), lambda i: (i, 0))
    return pl.pallas_call(
        update_kernel,
        grid=(row_blocks,),
        in_specs=[smem] * 3 + [strip] + [vmem] * 6,
        out_specs=strip,
        out_shape=jax.ShapeDtypeStruct(matrix.shape, matrix.dtype),
        scratch_shapes=[pltpu.VMEM((2, COL_CAP * BLK, BLK), jnp.bfloat16)],
        name="update",
    )(here, row_pattern, col_pattern, matrix, *in_vmem(*blocks))


def shards(matrix, row_pattern, col_pattern):
    prow = lax.axis_index(PROW).astype(jnp.int32)
    pcol = lax.axis_index("pcol").astype(jnp.int32)
    even = prow % 2 == 0
    here = jnp.where(jnp.arange(2) == 0, prow, pcol)
    first, rest, panel = pack(here, row_pattern, col_pattern, matrix)
    zero = jnp.zeros((), jnp.bfloat16)

    def tree(value, root, levels):
        held = jnp.where(root, value, zero)
        for level, letter in zip(levels, "abc"):
            source = value if letter == "a" else held
            for pairs in level:
                came = send(source, pairs)
                held = held + came
        return held

    first_held = tree(first, prow <= 1, SPREAD)
    rest_held = tree(rest, prow <= 1, SPREAD_REST)
    down_came = send(rest_held[: 2 * BLK], DOWN)
    up_came = send(jnp.concatenate([first_held, rest_held[2 * BLK :]], axis=0), UP)
    panel = tree(panel, pcol <= 1, [LINE_1, LINE_2])
    pivot_held = tree(first_held, pcol <= 1, [LINE_1, LINE_2])
    pivot_came = send(pivot_held, UP)
    mine = jnp.concatenate(
        [jnp.where(even, pivot_held, pivot_came), jnp.where(even, pivot_came, pivot_held), panel],
        axis=0,
    )
    other = send(mine, SWAP)
    lower_0, lower_1 = panels(here, row_pattern, mine, other)
    return update(
        here, row_pattern, col_pattern, matrix, lower_0, lower_1,
        first_held, rest_held, up_came, down_came,
    )


def solution(mesh):
    torus = Mesh(mesh.devices.reshape(X, Y, mesh.shape["pcol"]), AXES)
    placed = (P(PROW, "pcol"), P(), P())
    return jax.shard_map(
        shards, mesh=torus, in_specs=placed, out_specs=P(PROW, "pcol"), check_vma=False
    )
```
